512 devices in a mesh: gx: 32 (over z, core), gy: 16 (over y, x).
Axes of the slice: x: 4, y: 4, z: 16, core: 2. Of those that a mesh axis runs over, the one named last changes fastest.
Arguments:
- velocity: float32 [3, 6144, 8192], P(None, 'gx', 'gy'), may hold values from -6 to 6
- row_owner: int32 [32, 64], P('gx'), may hold values from 0 to 15, as said below
- cell_list: int32 [4, 262144], P(None, ('gx', 'gy')), may hold values from 0 to 786431, as said below
- weights: float32 [4, 262144], P(None, ('gx', 'gy')), may hold values from 0.05 to 0.5
- offsets: float32 [262144], P(('gx', 'gy')), may hold values from -0.5 to 0.5
- relax_rate: float32 [262144], P(('gx', 'gy')), may hold values from 0.05 to 0.8
- particle_velocity: float32 [3, 262144], P(None, ('gx', 'gy')), may hold values from -6 to 6
- live_counts: int32 [2048], P(('gx', 'gy')), may hold values from 1 to 128, as said below
Outputs:
- gradient: float32 [3, 6144, 8192], P(None, 'gx', 'gy')
- fluid_at_particle: float32 [3, 262144], P(None, ('gx', 'gy'))
- updated_velocity: float32 [3, 262144], P(None, ('gx', 'gy'))
The draws below stay inside these ranges and needn't reach their ends.
Inputs may be any that keep to these rules, and one draw needn't show every extreme that they name: `row_owner`: for every gx index and every gy index, at most 2 of that device's 4 row blocks name one owner; in every row of devices along gy one owner is named by exactly 2 blocks of every device; every owner is named by some block of the row. `cell_list`: every entry decodes as in the reference program to a block that exists; the 4 cells of one particle share q. `live_counts`: the live particles of a block are its first slots.
All inputs are finite; a program needn't handle non-finite values.
Results may differ from the reference program's by a relative error of at most 0.0029.
Values may be sent and summed in bfloat16 or wider, within the bound.
A program may use at most 128 MiB of HBM per device.

```python
import math
import jax
import jax.numpy as jnp

NX = 6144
CX = 192
LINES = 8192
ROWB = 128
NBLK_DEV = 4
NBLK = 64
CAP = 2
PART_DEV = 512
PSIZE = 128
PBLK_DEV = 4
PARTS_SIZE = 262144
STEN = 4
N_GX = 32
N_GY = 16
DEVICES = 512


def route_table(key):
    base_key = jax.random.fold_in(key, 7001)
    key_hot, key_order = jax.random.split(base_key)
    hot_owner = jax.random.randint(key_hot, (N_GX, 1, 1), 0, N_GY)
    sender = jnp.arange(N_GY)[None, :, None]
    position = jnp.arange(NBLK_DEV)[None, None, :]
    spread = (sender + position - CAP) % (N_GY - 1)
    owner_seq = jnp.where(position < CAP, hot_owner, (hot_owner + 1 + spread) % N_GY)
    owner_seq = jnp.broadcast_to(owner_seq, (N_GX, N_GY, NBLK_DEV))
    scores = jax.random.randint(key_order, (N_GX, N_GY, NBLK_DEV), 0, 1 << 20) * NBLK_DEV + position
    shuffle = jnp.argsort(scores, axis=-1)
    inverse = jnp.argsort(shuffle, axis=-1)
    routes = jnp.take_along_axis(owner_seq, inverse, -1)
    return (routes.reshape(N_GX, NBLK).astype(jnp.int32), hot_owner)


def draw_row_owner(key, part):
    routes, hot_owner = route_table(key)
    return routes


def draw_cell_list(key, part):
    routes, hot_owner = route_table(key)
    pick_key = jax.random.fold_in(key, 7002)
    key_block, key_line, key_cell = jax.random.split(pick_key, 3)
    particle_ids = jnp.arange(PARTS_SIZE)
    device_ids = particle_ids // PART_DEV
    column_ids = device_ids // N_GY
    owner_ids = device_ids % N_GY
    to_owner = (routes[column_ids] == owner_ids[:, None]).astype(jnp.int32)
    running = jnp.cumsum(to_owner, 1)
    available = running[:, -1]
    chosen_rank = jax.random.randint(key_block, (PARTS_SIZE,), 0, available)
    block_id = jnp.sum((running <= chosen_rank[:, None]).astype(jnp.int32), 1)
    sender = block_id // NBLK_DEV
    ordinal = jnp.arange(NBLK)[None, :]
    before = (ordinal < block_id[:, None]) & (ordinal >= (sender * NBLK_DEV)[:, None])
    within = jnp.sum(to_owner * before.astype(jnp.int32), 1)
    slot_ids = sender * CAP + within
    line_index = jax.random.randint(key_line, (PARTS_SIZE,), 0, ROWB)
    x_index = jax.random.randint(key_cell, (PARTS_SIZE,), 0, CX)
    top_particle = hot_owner[0, 0, 0] * PART_DEV
    slot_ids = slot_ids.at[top_particle].set(N_GY * CAP - 1).at[top_particle + 1].set(0)
    line_index = line_index.at[top_particle].set(ROWB - 1).at[top_particle + 1].set(0)
    x_index = x_index.at[top_particle].set(CX - 1).at[top_particle + 1].set(0)
    stencil = jnp.arange(STEN)[:, None]
    x_cells = (x_index[None] + stencil % 2) % CX
    line_cells = (line_index[None] + stencil // 2) % ROWB
    return ((slot_ids[None] * ROWB + line_cells) * CX + x_cells).astype(jnp.int32)


def draw_live_counts(key, part):
    base_key = jax.random.fold_in(key, 7003)
    key_level, key_raw = jax.random.split(base_key)
    load_level = jax.random.randint(key_level, (DEVICES, 1), 1, 5)
    raw_draw = jax.random.randint(key_raw, (DEVICES, PBLK_DEV), 0, PSIZE)
    counts = (1 + raw_draw * load_level // 4).reshape(-1)
    return counts.at[0].set(PSIZE).astype(jnp.int32)


def shard_levels(stream_key, extent, pieces, least, top_value):
    def one(axis_at, parts):
        draws = jax.random.uniform(jax.random.fold_in(jax.random.fold_in(stream_key, 6), axis_at), (parts,), jnp.float32, least / len(pieces), top_value / len(pieces))
        return jnp.repeat(jnp.exp(draws), extent[axis_at] // parts).reshape((-1,) + (1,) * (len(extent) - axis_at - 1))

    factor_of = one(*pieces[0])
    for cut in pieces[1:]:
        factor_of = factor_of * one(*cut)
    return factor_of


def normal_values(own_key, dims, deviation, reach, cuts=(), held_as=jnp.bfloat16):
    values = deviation * jax.random.normal(own_key, dims, jnp.float32)
    if cuts:
        values = values * shard_levels(own_key, dims, cuts, -0.22, 0.18)
    return jnp.clip(values, -reach, reach).astype(held_as)


def setup_inputs(seed: int = 0) -> dict:
    keys = jax.random.split(jax.random.key(seed), 9)
    velocity = normal_values(keys[0], (3, NX, LINES), 1.0, 6.0, ((1, 32), (2, 16)), jnp.float32)
    row_owner = draw_row_owner(jax.random.fold_in(keys[8], 71), 0)
    cell_list = draw_cell_list(jax.random.fold_in(keys[8], 71), 0)
    weights = jnp.clip(0.05 + 0.45 * jax.random.uniform(keys[3], (STEN, PARTS_SIZE), jnp.float32) ** shard_levels(keys[3], (STEN, PARTS_SIZE), ((1, 512),), -0.2, 0.2), 0.05, 0.5)
    offsets = jnp.clip(jax.random.uniform(keys[4], (PARTS_SIZE,), jnp.float32, -0.5, 0.5) * shard_levels(keys[4], (PARTS_SIZE,), ((0, 512),), -0.4, 0.0), -0.5, 0.5)
    relax_rate = jnp.clip(jnp.exp(math.log(0.8) - 2.7725887 * jax.random.uniform(keys[5], (PARTS_SIZE,), jnp.float32) ** shard_levels(keys[5], (PARTS_SIZE,), ((0, 512),), -0.2, 0.2)), 0.05, 0.8)
    particle_velocity = normal_values(keys[6], (3, PARTS_SIZE), 1.0, 6.0, ((1, 512),), jnp.float32)
    live_counts = draw_live_counts(jax.random.fold_in(keys[8], 71), 0)
    return {"velocity": velocity, "row_owner": row_owner, "cell_list": cell_list, "weights": weights, "offsets": offsets, "relax_rate": relax_rate, "particle_velocity": particle_velocity, "live_counts": live_counts}


def stencil_sum(values, weights, offsets):
    carried = values[:3].astype(jnp.float32)
    slopes = values[3:].astype(jnp.float32)
    return jnp.sum(weights[None] * (carried + offsets[None, None] * slopes), 1)


def reference(velocity, row_owner, cell_list, weights, offsets, relax_rate, particle_velocity, live_counts):
    wavenumber = 2.0 * math.pi * jnp.fft.fftfreq(NX)
    modified_wave = ((14.0 / 9.0) * jnp.sin(wavenumber) + (1.0 / 18.0) * jnp.sin(2.0 * wavenumber)) / (1.0 + (2.0 / 3.0) * jnp.cos(wavenumber))
    derivatives = []
    for channel in range(3):
        spectrum = jnp.fft.fft(velocity[channel], axis=0)
        derivatives.append(jnp.real(jnp.fft.ifft(1j * modified_wave[:, None] * spectrum, axis=0)).astype(jnp.float32))
    gradient = jnp.stack(derivatives)
    fields = jnp.concatenate([velocity, gradient], 0).astype(jnp.bfloat16)
    particle_ids = jnp.arange(PARTS_SIZE).astype(jnp.int32)
    device_ids = particle_ids // PART_DEV
    column_ids = device_ids // N_GY
    owner_ids = device_ids % N_GY
    x_index = cell_list % CX
    remainder = cell_list // CX
    line_index = remainder % ROWB
    slot_ids = remainder // ROWB
    sender = slot_ids // CAP
    within = slot_ids % CAP
    block_ids = sender[..., None] * NBLK_DEV + jnp.arange(NBLK_DEV).astype(jnp.int32)
    owners_seen = row_owner[column_ids[None, :, None], block_ids]
    running = jnp.cumsum((owners_seen == owner_ids[None, :, None]).astype(jnp.int32), -1)
    position = jnp.sum((running <= within[..., None]).astype(jnp.int32), -1)
    cell_line = (sender * NBLK_DEV + position) * ROWB + line_index
    cell_x = column_ids[None, :] * CX + x_index
    values = fields[:, cell_x, cell_line]
    raw = stencil_sum(values, weights, offsets)
    alive = (jnp.arange(PSIZE)[None, :] < live_counts[:, None]).reshape(PARTS_SIZE)
    fluid_at_particle = jnp.where(alive[None], raw, 0.0)
    updated_velocity = jnp.where(alive[None], particle_velocity + relax_rate[None] * (fluid_at_particle - particle_velocity), particle_velocity)
    return gradient, fluid_at_particle, updated_velocity
```

```python
import functools
import math

import jax
import jax.numpy as jnp
import numpy as np
from jax import lax
from jax.experimental import pallas as pl
from jax.experimental.pallas import tpu as pltpu
from jax.sharding import PartitionSpec as P

ROWB = 128
PSIZE = 128
CAP = 2
STEN = 4
XSPLIT = 4
MESH = pl.DeviceIdType.MESH

DECAY = (3.0 - math.sqrt(5.0)) / 2.0
RATIO = -DECAY
GAIN = 3.0 / math.sqrt(5.0)


def green(distance):
    return GAIN * RATIO ** abs(distance)


def response(d):
    return (7.0 / 9.0) * (green(d + 1) - green(d - 1)) + (1.0 / 36.0) * (green(d + 2) - green(d - 2))


TAIL = response(2) / RATIO**2
NEAR = response(1) - TAIL * RATIO


def response_matrix(x_cells):
    table = np.array([response(d) for d in range(1 - x_cells, x_cells)])
    position = np.arange(x_cells)
    exact = table[position[:, None] - position[None, :] + x_cells - 1]
    high = exact.astype(jnp.bfloat16)
    low = (exact - high.astype(np.float64)).astype(jnp.bfloat16)
    return np.stack([high, low])


def decay_table(x_cells):
    position = np.arange(x_cells)
    powers = RATIO ** np.minimum(position, x_cells - 1 - position).astype(np.float64)
    return np.broadcast_to(powers[:, None], (x_cells, ROWB)).astype(np.float32)


def third(value):
    return lax.shift_right_logical(value * 43691, 17)


def kernel(
    ring,
    side,
    owner_ref,
    vel_ref,
    cells_ref,
    weights_ref,
    offsets_ref,
    matrix_ref,
    decay_ref,
    grad,
    raw_ref,
    owners,
    vel,
    matrix,
    decay,
    fields,
    halo_out,
    halo_in,
    cells,
    weights,
    offsets,
    picked,
    back_out,
    back_in,
    load_sem,
    halo_send,
    halo_recv,
    cell_send,
    cell_recv,
    weight_send,
    weight_recv,
    offset_send,
    offset_recv,
    back_send,
    back_recv,
):
    components, x_cells, lines = vel.shape
    blocks = lines // ROWB
    half = x_cells // 2
    run = x_cells // XSPLIT
    particles = cells.shape[-1]
    peers = side * side
    col = lax.axis_index("gx")
    row = lax.axis_index("gy")
    row_y, row_x = lax.div(row, side), lax.rem(row, side)
    right, left = lax.rem(col + 1, ring), lax.rem(col + ring - 1, ring)

    def peer(step):
        y = lax.rem(row_y + lax.div(step, side), side)
        x = lax.rem(row_x + lax.rem(step, side), side)
        return y * side + x

    barrier = pltpu.get_barrier_semaphore()
    for neighbour in (left, right):
        pl.semaphore_signal(barrier, inc=1, device_id=(neighbour, row), device_id_type=MESH)

    @pl.loop(1, peers)
    def _(step):
        pl.semaphore_signal(barrier, inc=1, device_id=(col, peer(step)), device_id_type=MESH)

    loads = [
        pltpu.make_async_copy(source, target, load_sem.at[i])
        for i, (source, target) in enumerate(
            (
                (vel_ref, vel),
                (decay_ref, decay),
                (cells_ref, cells.at[0]),
                (weights_ref, weights.at[0]),
                (offsets_ref, offsets.at[0]),
                (matrix_ref, matrix),
                (owner_ref, owners),
            )
        )
    ]
    for load in loads:
        load.start()

    loads[0].wait()
    loads[1].wait()
    for c in range(components):
        for b in range(blocks):
            lanes = slice(b * ROWB, (b + 1) * ROWB)
            halo_out[0, c : c + 1, lanes] = jnp.sum(
                vel[c, half:, lanes] * decay[half:, :], 0, keepdims=True
            )
            halo_out[1, c : c + 1, lanes] = jnp.sum(
                vel[c, :half, lanes] * decay[:half, :], 0, keepdims=True
            )
        halo_out[0, 4 + c : 5 + c, :] = vel[c, x_cells - 1 : x_cells, :]
        halo_out[1, 4 + c : 5 + c, :] = vel[c, 0:1, :]
    for load in loads[2:]:
        load.wait()

    def halo_copy(way, target):
        return pltpu.make_async_remote_copy(
            src_ref=halo_out.at[way],
            dst_ref=halo_in.at[way],
            send_sem=halo_send.at[way],
            recv_sem=halo_recv.at[way],
            device_id=(target, row),
            device_id_type=MESH,
        )

    def share(array, step, send_sem, recv_sem):
        return pltpu.make_async_remote_copy(
            src_ref=array.at[0],
            dst_ref=array.at[step],
            send_sem=send_sem.at[step],
            recv_sem=recv_sem.at[step],
            device_id=(col, peer(step)),
            device_id_type=MESH,
        )

    def give_back(step):
        return pltpu.make_async_remote_copy(
            src_ref=back_out.at[step],
            dst_ref=back_in.at[step],
            send_sem=back_send.at[step],
            recv_sem=back_recv.at[step],
            device_id=(col, peer(step)),
            device_id_type=MESH,
        )

    shared = (
        (cells, cell_send, cell_recv),
        (weights, weight_send, weight_recv),
        (offsets, offset_send, offset_recv),
    )
    pl.semaphore_wait(barrier, peers + 1)
    halos = [halo_copy(0, right), halo_copy(1, left)]
    for halo in halos:
        halo.start()
    for entry in shared:

        @pl.loop(1, peers)
        def _(step, entry=entry):
            array, send_sem, recv_sem = entry
            share(array, step, send_sem, recv_sem).start()

    for c in range(components):
        value = vel[c]
        high = value.astype(jnp.bfloat16)
        low = (value - high.astype(jnp.float32)).astype(jnp.bfloat16)
        dot = functools.partial(jnp.dot, preferred_element_type=jnp.float32)
        grad[c] = dot(matrix[0], high) + (dot(matrix[0], low) + dot(matrix[1], high))
        for b in range(blocks):
            lanes = slice(b * ROWB, (b + 1) * ROWB)
            for k in range(XSPLIT):
                fields[b, c * run : (c + 1) * run, k * ROWB : (k + 1) * ROWB] = high[
                    k * run : (k + 1) * run, lanes
                ]

    for halo in halos:
        halo.wait_recv()
    for c in range(components):
        for end, way, sign in ((0, 0, 1.0), (x_cells - 1, 1, -1.0)):
            grad[c, end : end + 1, :] += (sign * NEAR) * halo_in[way, 4 + c : 5 + c, :]
        for b in range(blocks):
            lanes = slice(b * ROWB, (b + 1) * ROWB)
            for way, sign in ((0, 1.0), (1, -1.0)):
                rows = slice(way * half, (way + 1) * half)
                far = (sign * TAIL * RATIO) * halo_in[way, c : c + 1, lanes]
                total = grad[c, rows, lanes] + decay[rows, :] * far
                grad[c, rows, lanes] = total
                rounded = total.astype(jnp.bfloat16)
                for k in range(XSPLIT // 2):
                    place = way * (XSPLIT // 2) + k
                    fields[
                        b,
                        (components + c) * run : (components + c + 1) * run,
                        place * ROWB : (place + 1) * ROWB,
                    ] = rounded[k * run : (k + 1) * run]

    for array, send_sem, recv_sem in shared:

        @pl.loop(1, peers)
        def _(step, entry=(array, send_sem, recv_sem)):
            array, send_sem, recv_sem = entry
            share(array, step, send_sem, recv_sem).wait()

    owner_of = [owners[0, row * blocks + b] for b in range(blocks)]
    depth = XSPLIT * ROWB
    place_id = lax.broadcasted_iota(jnp.int32, (256, particles), 0).astype(jnp.bfloat16)
    run_id = lax.broadcasted_iota(jnp.int32, (run, particles), 0)
    one, zero = jnp.ones((), jnp.bfloat16), jnp.zeros((), jnp.bfloat16)

    @pl.loop(0, blocks)
    def _(b):
        owner = owners[0, row * blocks + b]
        rank = jnp.int32(0)
        for other in range(blocks):
            same = jnp.where(owner_of[other] == owner, 1, 0)
            rank += same * jnp.where(other < b, 1, 0)
        slot_y = lax.rem(row_y - lax.div(owner, side) + side, side)
        slot_x = lax.rem(row_x - lax.rem(owner, side) + side, side)
        slot = slot_y * side + slot_x
        cell = cells[slot]
        weight = weights[slot]
        offset = offsets[slot]
        line = third(lax.shift_right_logical(cell, 6))
        x = cell - line * x_cells
        source = lax.shift_right_logical(line, 7)
        line = line & (ROWB - 1)
        part = third(lax.shift_right_logical(x, (run // 3).bit_length() - 1))
        within = x - part * run
        place = part * ROWB + line
        sums = [jnp.zeros((8, particles), jnp.float32) for _ in range(components)]
        table = fields[b]
        for s in range(STEN):
            hot = []
            for start in range(0, depth, 256):
                key = (place[s : s + 1] - start).astype(jnp.bfloat16)
                hot.append(jnp.where(place_id == key, one, zero))
            values = jnp.dot(
                table, jnp.concatenate(hot, 0), preferred_element_type=jnp.float32
            )
            chosen = run_id == within[s : s + 1]
            parts = []
            for f in range(2 * components):
                kept = jnp.where(chosen, values[f * run : (f + 1) * run], 0.0)
                parts.append(jnp.sum(kept.reshape(run // 8, 8, particles), 0))
            for c in range(components):
                sums[c] += weight[s : s + 1] * (parts[c] + offset * parts[components + c])
        mine = source[0:1] == row * CAP + rank
        for c in range(components):
            total = jnp.sum(sums[c], 0, keepdims=True)
            picked[b, c : c + 1, :] = jnp.where(mine, total, 0.0)

    @pl.loop(0, peers)
    def _(step):
        to = peer(step)
        total = jnp.zeros(picked.shape[1:], jnp.float32)
        for b in range(blocks):
            total += picked[b] * jnp.where(owner_of[b] == to, 1.0, 0.0)
        back_out[step] = total

    @pl.loop(1, peers)
    def _(step):
        give_back(step).start()

    @pl.loop(1, peers)
    def _(step):
        give_back(step).wait()

    total = back_out[0]
    for step in range(1, peers):
        total += back_in[step]
    raw_ref[...] = total
    for halo in halos:
        halo.wait_send()


def per_device(
    ring,
    side,
    velocity,
    row_owner,
    cell_list,
    weights,
    offsets,
    relax_rate,
    particle_velocity,
    live_counts,
):
    components, x_cells, lines = velocity.shape
    blocks = lines // ROWB
    particles = weights.shape[1]
    peers = side * side
    run = x_cells // XSPLIT
    far = pl.BlockSpec(memory_space=pltpu.HBM)
    near = pl.BlockSpec(memory_space=pltpu.VMEM)
    dma = pltpu.SemaphoreType.DMA
    gradient, raw = pl.pallas_call(
        functools.partial(kernel, ring, side),
        out_shape=(
            jax.ShapeDtypeStruct(velocity.shape, jnp.float32),
            jax.ShapeDtypeStruct((components, particles), jnp.float32),
        ),
        in_specs=[far] * 7,
        out_specs=(near, near),
        scratch_shapes=[
            pltpu.SMEM(row_owner.shape, jnp.int32),
            pltpu.VMEM(velocity.shape, jnp.float32),
            pltpu.VMEM((2, x_cells, x_cells), jnp.bfloat16),
            pltpu.VMEM((x_cells, ROWB), jnp.float32),
            pltpu.VMEM((blocks, 2 * components * run, XSPLIT * ROWB), jnp.bfloat16),
            pltpu.VMEM((2, 8, lines), jnp.float32),
            pltpu.VMEM((2, 8, lines), jnp.float32),
            pltpu.VMEM((peers, STEN, particles), jnp.int32),
            pltpu.VMEM((peers, STEN, particles), jnp.float32),
            pltpu.VMEM((peers, 1, particles), jnp.float32),
            pltpu.VMEM((blocks, components, particles), jnp.float32),
            pltpu.VMEM((peers, components, particles), jnp.float32),
            pltpu.VMEM((peers, components, particles), jnp.float32),
            dma((7,)),
            dma((2,)),
            dma((2,)),
        ]
        + [dma((peers,))] * 8,
        compiler_params=pltpu.CompilerParams(
            collective_id=0, has_side_effects=True, vmem_limit_bytes=48 * 1024 * 1024
        ),
    )(
        *(
            pltpu.with_memory_space_constraint(array, pltpu.HBM)
            for array in (
                row_owner,
                velocity,
                cell_list,
                weights,
                offsets[None],
                jnp.asarray(response_matrix(x_cells)),
                jnp.asarray(decay_table(x_cells)),
            )
        ),
    )
    alive = (jnp.arange(PSIZE)[None, :] < live_counts[:, None]).reshape(particles)
    fluid_at_particle = jnp.where(alive[None], raw, 0.0)
    updated_velocity = jnp.where(
        alive[None],
        particle_velocity + relax_rate[None] * (fluid_at_particle - particle_velocity),
        particle_velocity,
    )
    return gradient, fluid_at_particle, updated_velocity


def solution(mesh):
    side = math.isqrt(mesh.shape["gy"])
    return jax.shard_map(
        functools.partial(per_device, mesh.shape["gx"], side),
        mesh=mesh,
        in_specs=(
            P(None, "gx", "gy"),
            P("gx", None),
            P(None, ("gx", "gy")),
            P(None, ("gx", "gy")),
            P(("gx", "gy")),
            P(("gx", "gy")),
            P(None, ("gx", "gy")),
            P(("gx", "gy")),
        ),
        out_specs=(P(None, "gx", "gy"), P(None, ("gx", "gy")), P(None, ("gx", "gy"))),
        check_vma=False,
    )
```

```python
import functools
import math

import jax
import jax.numpy as jnp
import numpy as np
from jax import lax
from jax.experimental import pallas as pl
from jax.experimental.pallas import tpu as pltpu
from jax.sharding import PartitionSpec as P

ROWB = 128
PSIZE = 128
CAP = 2
STEN = 4
XSPLIT = 4
MESH = pl.DeviceIdType.MESH

DECAY = (3.0 - math.sqrt(5.0)) / 2.0
RATIO = -DECAY
GAIN = 3.0 / math.sqrt(5.0)


def green(distance):
    return GAIN * RATIO ** abs(distance)


def response(d):
    return (7.0 / 9.0) * (green(d + 1) - green(d - 1)) + (1.0 / 36.0) * (green(d + 2) - green(d - 2))


TAIL = response(2) / RATIO**2
NEAR = response(1) - TAIL * RATIO


def response_matrix(x_cells):
    table = np.array([response(d) for d in range(1 - x_cells, x_cells)])
    position = np.arange(x_cells)
    exact = table[position[:, None] - position[None, :] + x_cells - 1]
    high = exact.astype(jnp.bfloat16)
    low = (exact - high.astype(np.float64)).astype(jnp.bfloat16)
    return np.stack([high, low])


def decay_table(x_cells):
    position = np.arange(x_cells)
    powers = RATIO ** np.minimum(position, x_cells - 1 - position).astype(np.float64)
    return np.broadcast_to(powers[:, None], (x_cells, ROWB)).astype(np.float32)


def third(value):
    return lax.shift_right_logical(value * 43691, 17)


def is_equal(value, other):
    return jnp.where(value == other, 1, 0)


def kernel(
    ring,
    side,
    owner_ref,
    vel_ref,
    cells_ref,
    weights_ref,
    offsets_ref,
    relax_ref,
    particle_ref,
    live_ref,
    matrix_ref,
    decay_ref,
    grad,
    fluid,
    updated,
    owners,
    vel,
    matrix,
    decay,
    carried,
    slopes,
    hot,
    halo_out,
    halo_in,
    cells,
    weights,
    offsets,
    relax,
    particle,
    live,
    picked,
    result,
    back_out,
    back_in,
    ready,
    load_sem,
    halo_send,
    halo_recv,
    cell_send,
    cell_recv,
    weight_send,
    weight_recv,
    offset_send,
    offset_recv,
    back_send,
    back_recv,
):
    components, x_cells, lines = vel.shape
    blocks = lines // ROWB
    run = x_cells // XSPLIT
    particles = cells.shape[-1]
    peers = side * side
    col = lax.axis_index("gx")
    row = lax.axis_index("gy")
    row_y, row_x = lax.div(row, side), lax.rem(row, side)
    right, left = lax.rem(col + 1, ring), lax.rem(col + ring - 1, ring)

    def peer(step):
        y = lax.rem(row_y + lax.div(step, side), side)
        x = lax.rem(row_x + lax.rem(step, side), side)
        return y * side + x

    near_first = sorted(range(1, side), key=lambda k: -min(k, side - k))

    odd = lax.rem(col, 2)
    first, last, second = is_equal(col, 0), is_equal(col, ring - 1), is_equal(col, 1)
    leads = (
        first + odd * (1 - last) * (1 - first),
        first + odd * (1 - second) * (1 - first),
    )
    beside = (right, left)

    barrier = pltpu.get_barrier_semaphore()

    for k in near_first:
        for step in (k, k * side):
            pl.semaphore_signal(
                barrier, inc=1, device_id=(col, peer(step)), device_id_type=MESH
            )
    for way in range(2):

        @pl.when(leads[way] == 1)
        def _(way=way):
            pl.semaphore_signal(
                barrier, inc=1, device_id=(beside[way], row), device_id_type=MESH
            )

    edge = (slice(0, run), slice(x_cells - run, x_cells))
    inner = slice(run, x_cells - run)
    loads = [
        pltpu.make_async_copy(source, target, load_sem.at[i])
        for i, (source, target) in enumerate(
            (
                (decay_ref, decay),
                (vel_ref.at[:, edge[0]], vel.at[:, edge[0]]),
                (vel_ref.at[:, edge[1]], vel.at[:, edge[1]]),
                (cells_ref, cells.at[0, 0]),
                (weights_ref, weights.at[0, 0]),
                (offsets_ref, offsets.at[0, 0]),
                (vel_ref.at[:, inner], vel.at[:, inner]),
                (matrix_ref, matrix),
                (owner_ref, owners),
                (relax_ref, relax),
                (particle_ref, particle),
                (live_ref, live),
            )
        )
    ]
    for load in loads:
        load.start()

    def halo_copy(way):
        return pltpu.make_async_remote_copy(
            src_ref=halo_out.at[way],
            dst_ref=halo_in.at[way],
            send_sem=halo_send.at[way],
            recv_sem=halo_recv.at[way],
            device_id=(beside[way], row),
            device_id_type=MESH,
        )

    def share(entry, k):
        source, array, first, send_sem, recv_sem = entry
        return pltpu.make_async_remote_copy(
            src_ref=source,
            dst_ref=array.at[0, k],
            send_sem=send_sem.at[0, k],
            recv_sem=recv_sem.at[0, k],
            device_id=(col, peer(k * first)),
            device_id_type=MESH,
        )

    def share_line(entry, k):
        _, array, first, send_sem, recv_sem = entry
        return pltpu.make_async_remote_copy(
            src_ref=array.at[0],
            dst_ref=array.at[k],
            send_sem=send_sem.at[1, k],
            recv_sem=recv_sem.at[1, k],
            device_id=(col, peer(k * side // first)),
            device_id_type=MESH,
        )

    def give_back(step):
        return pltpu.make_async_remote_copy(
            src_ref=back_out.at[step],
            dst_ref=back_in.at[step],
            send_sem=back_send.at[step],
            recv_sem=back_recv.at[step],
            device_id=(col, peer(step)),
            device_id_type=MESH,
        )

    def hops(step):
        return sum(min(k, side - k) for k in divmod(step, side))

    farthest_first = sorted(range(1, peers), key=hops, reverse=True)
    shared = (
        (cells_ref, cells, 1, cell_send, cell_recv),
        (weights_ref, weights, side, weight_send, weight_recv),
        (offsets_ref, offsets, side, offset_send, offset_recv),
    )
    pl.semaphore_wait(barrier, 2 * (side - 1) + 2 - leads[0] - leads[1])
    for entry in shared:
        for k in near_first:
            share(entry, k).start()
    for way in range(2):

        @pl.when(leads[way] == 0)
        def _(way=way):
            pl.semaphore_signal(
                ready.at[1 - way], inc=1, device_id=(beside[way], row), device_id_type=MESH
            )

    for load in loads[:3]:
        load.wait()
    for c in range(components):
        for b in range(blocks):
            lanes = slice(b * ROWB, (b + 1) * ROWB)
            for way in range(2):
                rows = edge[1 - way]
                halo_out[way, c : c + 1, lanes] = jnp.sum(
                    vel[c, rows, lanes] * decay[rows, :], 0, keepdims=True
                )
        halo_out[0, 4 + c : 5 + c, :] = vel[c, x_cells - 1 : x_cells, :]
        halo_out[1, 4 + c : 5 + c, :] = vel[c, 0:1, :]

    for way in range(2):

        @pl.when(leads[way] == 0)
        def _(way=way):
            halo_copy(way).start()

    for load in loads[3:6]:
        load.wait()
    for entry in shared:
        for k in near_first:
            share(entry, k).wait_recv()
        for k in near_first:
            share_line(entry, k).start()

    for way in range(2):

        @pl.when(leads[way] == 1)
        def _(way=way):
            pl.semaphore_wait(ready.at[way], 1)
            halo_copy(way).start()

    for load in loads[6:]:
        load.wait()
    for c in range(components):
        value = vel[c]
        high = value.astype(jnp.bfloat16)
        low = (value - high.astype(jnp.float32)).astype(jnp.bfloat16)
        dot = functools.partial(jnp.dot, preferred_element_type=jnp.float32)
        total = dot(matrix[0], high) + (dot(matrix[0], low) + dot(matrix[1], high))
        grad[c] = total
        rounded = total.astype(jnp.bfloat16)
        for b in range(blocks):
            lanes = slice(b * ROWB, (b + 1) * ROWB)
            for part in range(XSPLIT):
                rows = slice(part * run, (part + 1) * run)
                place = slice(part * ROWB, (part + 1) * ROWB)
                carried[b, c * run : (c + 1) * run, place] = high[rows, lanes]
                if 0 < part < XSPLIT - 1:
                    slopes[b, c * run : (c + 1) * run, place] = rounded[rows, lanes]

    for entry in shared:
        for k in near_first:
            share_line(entry, k).wait_recv()

    owner_of = [owners[0, row * blocks + b] for b in range(blocks)]
    depth = 2 * ROWB
    place_id = lax.broadcasted_iota(jnp.int32, (depth, particles), 0).astype(jnp.bfloat16)
    run_id = lax.broadcasted_iota(jnp.int32, (run, particles), 0)
    one, zero = jnp.ones((), jnp.bfloat16), jnp.zeros((), jnp.bfloat16)

    def steps_from(owner):
        slot_y = lax.rem(row_y - lax.div(owner, side) + side, side)
        slot_x = lax.rem(row_x - lax.rem(owner, side) + side, side)
        return slot_y, slot_x

    def chosen(values, within):
        here = run_id == within
        parts = []
        for f in range(components):
            kept = jnp.where(here, values[f * run : (f + 1) * run], 0.0)
            parts.append(jnp.sum(kept.reshape(run // 8, 8, particles), 0))
        return parts

    def decode(cell):
        line = third(lax.shift_right_logical(cell, 6))
        x = cell - line * x_cells
        source = lax.shift_right_logical(line, 7)
        line = line & (ROWB - 1)
        part = third(lax.shift_right_logical(x, (run // 3).bit_length() - 1))
        within = x - part * run
        return source, part * ROWB + line, within

    @pl.loop(0, blocks)
    def _(b):
        slot_y, slot_x = steps_from(owners[0, row * blocks + b])
        source, place, within = decode(cells[slot_y, slot_x])
        weight = weights[slot_x, slot_y]
        sums = [jnp.zeros((8, particles), jnp.float32) for _ in range(components)]
        for s in range(STEN):
            ones = []
            for start in range(0, XSPLIT * ROWB, depth):
                key = (place[s : s + 1] - start).astype(jnp.bfloat16)
                ones.append(jnp.where(place_id == key, one, zero))
            ones = jnp.concatenate(ones, 0)
            hot[b * STEN + s] = ones
            values = jnp.dot(carried[b], ones, preferred_element_type=jnp.float32)
            value = chosen(values, within[s : s + 1])
            for c in range(components):
                sums[c] += weight[s : s + 1] * value[c]
        for c in range(components):
            picked[b, c] = sums[c]

    for way in range(2):
        halo_copy(way).wait_recv()
    for c in range(components):
        for way, end, sign in ((0, 0, 1.0), (1, x_cells - 1, -1.0)):
            grad[c, end : end + 1, :] += (sign * NEAR) * halo_in[way, 4 + c : 5 + c, :]
            for b in range(blocks):
                lanes = slice(b * ROWB, (b + 1) * ROWB)
                far = (sign * TAIL * RATIO) * halo_in[way, c : c + 1, lanes]
                total = grad[c, edge[way], lanes] + decay[edge[way], :] * far
                grad[c, edge[way], lanes] = total
                part = way * (XSPLIT - 1)
                slopes[b, c * run : (c + 1) * run, part * ROWB : (part + 1) * ROWB] = total.astype(
                    jnp.bfloat16
                )

    @pl.loop(0, blocks)
    def _(b):
        owner = owners[0, row * blocks + b]
        rank = jnp.int32(0)
        for other in range(blocks):
            same = jnp.where(owner_of[other] == owner, 1, 0)
            rank += same * jnp.where(other < b, 1, 0)
        slot_y, slot_x = steps_from(owner)
        source, _, within = decode(cells[slot_y, slot_x])
        weight = weights[slot_x, slot_y] * offsets[slot_x, slot_y]
        sums = [picked[b, c] for c in range(components)]
        for s in range(STEN):
            values = jnp.dot(
                slopes[b], hot[b * STEN + s], preferred_element_type=jnp.float32
            )
            slope = chosen(values, within[s : s + 1])
            for c in range(components):
                sums[c] += weight[s : s + 1] * slope[c]
        mine = source[0:1] == row * CAP + rank
        for c in range(components):
            total = jnp.sum(sums[c], 0, keepdims=True)
            result[b, c : c + 1, :] = jnp.where(mine, total, 0.0)

    for step in [*farthest_first, 0]:
        to = peer(step)
        total = jnp.zeros(result.shape[1:], jnp.float32)
        for b in range(blocks):
            total += result[b] * jnp.where(owner_of[b] == to, 1.0, 0.0)
        back_out[step] = total
    for step in farthest_first:
        give_back(step).start()

    @pl.loop(1, peers)
    def _(step):
        give_back(step).wait()

    total = back_out[0]
    for step in range(1, peers):
        total += back_in[step]
    lane = lax.broadcasted_iota(jnp.int32, (1, PSIZE), 1)
    alive = jnp.concatenate(
        [jnp.where(lane < live[0, k], 1, 0) for k in range(particles // PSIZE)], 1
    )
    old = particle[...]
    total = jnp.where(alive == 1, total, 0.0)
    fluid[...] = total
    updated[...] = jnp.where(alive == 1, old + relax[...] * (total - old), old)
    for way in range(2):
        halo_copy(way).wait_send()
    for entry in shared:
        for k in near_first:
            share(entry, k).wait_send()
            share_line(entry, k).wait_send()


def put_out(grad, fluid, updated, grad_out, fluid_out, updated_out, sems):
    copies = [pltpu.make_async_copy(grad.at[c], grad_out.at[c], sems.at[c]) for c in range(3)]
    copies.append(pltpu.make_async_copy(fluid, fluid_out, sems.at[3]))
    copies.append(pltpu.make_async_copy(updated, updated_out, sems.at[4]))
    for copy in copies:
        copy.start()
    for copy in copies:
        copy.wait()


def per_device(
    ring,
    side,
    velocity,
    row_owner,
    cell_list,
    weights,
    offsets,
    relax_rate,
    particle_velocity,
    live_counts,
):
    components, x_cells, lines = velocity.shape
    blocks = lines // ROWB
    particles = weights.shape[1]
    peers = side * side
    run = x_cells // XSPLIT
    far = pl.BlockSpec(memory_space=pltpu.HBM)
    near = pl.BlockSpec(memory_space=pltpu.VMEM)
    dma = pltpu.SemaphoreType.DMA
    results = pl.pallas_call(
        functools.partial(kernel, ring, side),
        out_shape=(
            jax.ShapeDtypeStruct(velocity.shape, jnp.float32),
            jax.ShapeDtypeStruct((components, particles), jnp.float32),
            jax.ShapeDtypeStruct((components, particles), jnp.float32),
        ),
        in_specs=[far] * 10,
        out_specs=(near, near, near),
        scratch_shapes=[
            pltpu.SMEM(row_owner.shape, jnp.int32),
            pltpu.VMEM(velocity.shape, jnp.float32),
            pltpu.VMEM((2, x_cells, x_cells), jnp.bfloat16),
            pltpu.VMEM((x_cells, ROWB), jnp.float32),
            pltpu.VMEM((blocks, components * run, XSPLIT * ROWB), jnp.bfloat16),
            pltpu.VMEM((blocks, components * run, XSPLIT * ROWB), jnp.bfloat16),
            pltpu.VMEM((blocks * STEN, XSPLIT * ROWB, particles), jnp.bfloat16),
            pltpu.VMEM((2, 8, lines), jnp.float32),
            pltpu.VMEM((2, 8, lines), jnp.float32),
            pltpu.VMEM((side, side, STEN, particles), jnp.int32),
            pltpu.VMEM((side, side, STEN, particles), jnp.float32),
            pltpu.VMEM((side, side, 1, particles), jnp.float32),
            pltpu.VMEM((1, particles), jnp.float32),
            pltpu.VMEM((components, particles), jnp.float32),
            pltpu.SMEM((1, particles // PSIZE), jnp.int32),
            pltpu.VMEM((blocks, components, 8, particles), jnp.float32),
            pltpu.VMEM((blocks, components, particles), jnp.float32),
            pltpu.VMEM((peers, components, particles), jnp.float32),
            pltpu.VMEM((peers, components, particles), jnp.float32),
            pltpu.SemaphoreType.REGULAR((2,)),
            dma((12,)),
            dma((2,)),
            dma((2,)),
        ]
        + [dma((2, side))] * 6
        + [dma((peers,))] * 2,
        compiler_params=pltpu.CompilerParams(
            collective_id=0, has_side_effects=True, vmem_limit_bytes=48 * 1024 * 1024
        ),
    )(
        *(
            pltpu.with_memory_space_constraint(array, pltpu.HBM)
            for array in (
                row_owner,
                velocity,
                cell_list,
                weights,
                offsets[None],
                relax_rate[None],
                particle_velocity,
                live_counts[None],
                jnp.asarray(response_matrix(x_cells)),
                jnp.asarray(decay_table(x_cells)),
            )
        ),
    )
    return pl.pallas_call(
        put_out,
        out_shape=tuple(jax.ShapeDtypeStruct(r.shape, r.dtype) for r in results),
        in_specs=[pl.BlockSpec(memory_space=pl.ANY)] * 3,
        out_specs=(far,) * 3,
        scratch_shapes=[dma((5,))],
        compiler_params=pltpu.CompilerParams(vmem_limit_bytes=4 * 1024 * 1024),
    )(*results)


def solution(mesh):
    side = math.isqrt(mesh.shape["gy"])
    return jax.shard_map(
        functools.partial(per_device, mesh.shape["gx"], side),
        mesh=mesh,
        in_specs=(
            P(None, "gx", "gy"),
            P("gx", None),
            P(None, ("gx", "gy")),
            P(None, ("gx", "gy")),
            P(("gx", "gy")),
            P(("gx", "gy")),
            P(None, ("gx", "gy")),
            P(("gx", "gy")),
        ),
        out_specs=(P(None, "gx", "gy"), P(None, ("gx", "gy")), P(None, ("gx", "gy"))),
        check_vma=False,
    )
```

```python
import functools
import math

import jax
import jax.numpy as jnp
import numpy as np
from jax import lax
from jax.experimental import pallas as pl
from jax.experimental.pallas import tpu as pltpu
from jax.sharding import PartitionSpec as P

ROWB = 128
PSIZE = 128
CAP = 2
STEN = 4
XSPLIT = 4
PIECES = 4
MESH = pl.DeviceIdType.MESH

DECAY = (3.0 - math.sqrt(5.0)) / 2.0
RATIO = -DECAY
GAIN = 3.0 / math.sqrt(5.0)


def green(distance):
    return GAIN * RATIO ** abs(distance)


def response(d):
    return (7.0 / 9.0) * (green(d + 1) - green(d - 1)) + (1.0 / 36.0) * (green(d + 2) - green(d - 2))


TAIL = response(2) / RATIO**2
NEAR = response(1) - TAIL * RATIO


def response_matrix(x_cells):
    table = np.array([response(d) for d in range(1 - x_cells, x_cells)])
    position = np.arange(x_cells)
    exact = table[position[:, None] - position[None, :] + x_cells - 1]
    high = exact.astype(jnp.bfloat16)
    low = (exact - high.astype(np.float64)).astype(jnp.bfloat16)
    return np.stack([high, low])


def decay_table(x_cells):
    position = np.arange(x_cells)
    powers = RATIO ** np.minimum(position, x_cells - 1 - position).astype(np.float64)
    return np.broadcast_to(powers[:, None], (x_cells, ROWB)).astype(np.float32)


def third(value):
    return lax.shift_right_logical(value * 43691, 17)


def is_equal(value, other):
    return jnp.where(value == other, 1, 0)


def kernel(
    ring,
    side,
    owner_ref,
    vel_ref,
    cells_ref,
    weights_ref,
    offsets_ref,
    relax_ref,
    particle_ref,
    live_ref,
    matrix_ref,
    decay_ref,
    grad,
    fluid,
    updated,
    owners,
    vel,
    matrix,
    decay,
    fields,
    halo_out,
    halo_in,
    cells,
    weights,
    offsets,
    relax,
    particle,
    live,
    result,
    back_out,
    back_in,
    ready,
    load_sem,
    halo_send,
    halo_recv,
    cell_send,
    cell_recv,
    weight_send,
    weight_recv,
    offset_send,
    offset_recv,
    back_send,
    back_recv,
):
    components, x_cells, lines = vel.shape
    blocks = lines // ROWB
    run = x_cells // XSPLIT
    particles = cells.shape[-1]
    peers = side * side
    col = lax.axis_index("gx")
    row = lax.axis_index("gy")
    row_y, row_x = lax.div(row, side), lax.rem(row, side)
    right, left = lax.rem(col + 1, ring), lax.rem(col + ring - 1, ring)

    def peer(step):
        y = lax.rem(row_y + lax.div(step, side), side)
        x = lax.rem(row_x + lax.rem(step, side), side)
        return y * side + x

    near_first = sorted(range(1, side), key=lambda k: -min(k, side - k))

    odd = lax.rem(col, 2)
    first, last, second = is_equal(col, 0), is_equal(col, ring - 1), is_equal(col, 1)
    leads = (
        first + odd * (1 - last) * (1 - first),
        first + odd * (1 - second) * (1 - first),
    )
    beside = (right, left)

    barrier = pltpu.get_barrier_semaphore()

    for k in near_first:
        for step in (k, k * side):
            pl.semaphore_signal(
                barrier, inc=1, device_id=(col, peer(step)), device_id_type=MESH
            )
    for way in range(2):

        @pl.when(leads[way] == 1)
        def _(way=way):
            pl.semaphore_signal(
                barrier, inc=1, device_id=(beside[way], row), device_id_type=MESH
            )

    edge = (slice(0, run), slice(x_cells - run, x_cells))
    inner = slice(run, x_cells - run)
    loads = [
        pltpu.make_async_copy(source, target, load_sem.at[i])
        for i, (source, target) in enumerate(
            (
                (decay_ref, decay),
                (vel_ref.at[:, edge[0]], vel.at[:, edge[0]]),
                (vel_ref.at[:, edge[1]], vel.at[:, edge[1]]),
                (cells_ref, cells.at[0, 0]),
                (weights_ref, weights.at[0, 0]),
                (offsets_ref, offsets.at[0, 0]),
                (vel_ref.at[:, inner], vel.at[:, inner]),
                (matrix_ref, matrix),
                (owner_ref, owners),
                (relax_ref, relax),
                (particle_ref, particle),
                (live_ref, live),
            )
        )
    ]
    for load in loads:
        load.start()

    def halo_copy(way):
        return pltpu.make_async_remote_copy(
            src_ref=halo_out.at[way],
            dst_ref=halo_in.at[way],
            send_sem=halo_send.at[way],
            recv_sem=halo_recv.at[way],
            device_id=(beside[way], row),
            device_id_type=MESH,
        )

    def share(entry, k):
        source, array, first, send_sem, recv_sem = entry
        return pltpu.make_async_remote_copy(
            src_ref=source,
            dst_ref=array.at[0, k],
            send_sem=send_sem.at[0, k],
            recv_sem=recv_sem.at[0, k],
            device_id=(col, peer(k * first)),
            device_id_type=MESH,
        )

    def share_line(entry, k):
        _, array, first, send_sem, recv_sem = entry
        return pltpu.make_async_remote_copy(
            src_ref=array.at[0],
            dst_ref=array.at[k],
            send_sem=send_sem.at[1, k],
            recv_sem=recv_sem.at[1, k],
            device_id=(col, peer(k * side // first)),
            device_id_type=MESH,
        )

    def give_back(step):
        return pltpu.make_async_remote_copy(
            src_ref=back_out.at[step],
            dst_ref=back_in.at[step],
            send_sem=back_send.at[step],
            recv_sem=back_recv.at[step],
            device_id=(col, peer(step)),
            device_id_type=MESH,
        )

    def hops(step):
        return sum(min(k, side - k) for k in divmod(step, side))

    farthest_first = sorted(range(1, peers), key=hops, reverse=True)
    shared = (
        (cells_ref, cells, 1, cell_send, cell_recv),
        (weights_ref, weights, side, weight_send, weight_recv),
        (offsets_ref, offsets, side, offset_send, offset_recv),
    )
    pl.semaphore_wait(barrier, 2 * (side - 1) + 2 - leads[0] - leads[1])
    for entry in shared:
        for k in near_first:
            share(entry, k).start()
    for way in range(2):

        @pl.when(leads[way] == 0)
        def _(way=way):
            pl.semaphore_signal(
                ready.at[1 - way], inc=1, device_id=(beside[way], row), device_id_type=MESH
            )

    for load in loads[:3]:
        load.wait()
    for c in range(components):
        for b in range(blocks):
            lanes = slice(b * ROWB, (b + 1) * ROWB)
            for way in range(2):
                rows = edge[1 - way]
                halo_out[way, c : c + 1, lanes] = jnp.sum(
                    vel[c, rows, lanes] * decay[rows, :], 0, keepdims=True
                )
        halo_out[0, 4 + c : 5 + c, :] = vel[c, x_cells - 1 : x_cells, :]
        halo_out[1, 4 + c : 5 + c, :] = vel[c, 0:1, :]

    for way in range(2):

        @pl.when(leads[way] == 0)
        def _(way=way):
            halo_copy(way).start()

    for load in loads[3:6]:
        load.wait()
    for entry in shared:
        for k in near_first:
            share(entry, k).wait_recv()
        for k in near_first:
            share_line(entry, k).start()

    for way in range(2):

        @pl.when(leads[way] == 1)
        def _(way=way):
            pl.semaphore_wait(ready.at[way], 1)
            halo_copy(way).start()

    for load in loads[6:]:
        load.wait()
    for c in range(components):
        value = vel[c]
        high = value.astype(jnp.bfloat16)
        low = (value - high.astype(jnp.float32)).astype(jnp.bfloat16)
        dot = functools.partial(jnp.dot, preferred_element_type=jnp.float32)
        total = dot(matrix[0], high) + (dot(matrix[0], low) + dot(matrix[1], high))
        grad[c] = total
        rounded = total.astype(jnp.bfloat16)
        for b in range(blocks):
            lanes = slice(b * ROWB, (b + 1) * ROWB)
            for part in range(XSPLIT):
                rows = slice(part * run, (part + 1) * run)
                place = slice(part * ROWB, (part + 1) * ROWB)
                fields[b, c * run : (c + 1) * run, place] = high[rows, lanes]
                if 0 < part < XSPLIT - 1:
                    d = components + c
                    fields[b, d * run : (d + 1) * run, place] = rounded[rows, lanes]

    for way in range(2):
        halo_copy(way).wait_recv()
    for c in range(components):
        for way, end, sign in ((0, 0, 1.0), (1, x_cells - 1, -1.0)):
            grad[c, end : end + 1, :] += (sign * NEAR) * halo_in[way, 4 + c : 5 + c, :]
            for b in range(blocks):
                lanes = slice(b * ROWB, (b + 1) * ROWB)
                far = (sign * TAIL * RATIO) * halo_in[way, c : c + 1, lanes]
                total = grad[c, edge[way], lanes] + decay[edge[way], :] * far
                grad[c, edge[way], lanes] = total
                part = way * (XSPLIT - 1)
                d = components + c
                fields[b, d * run : (d + 1) * run, part * ROWB : (part + 1) * ROWB] = total.astype(
                    jnp.bfloat16
                )

    for entry in shared:
        for k in near_first:
            share_line(entry, k).wait_recv()

    owner_of = [owners[0, row * blocks + b] for b in range(blocks)]
    depth = 2 * ROWB
    place_id = lax.broadcasted_iota(jnp.int32, (depth, particles), 0).astype(jnp.bfloat16)
    run_id = lax.broadcasted_iota(jnp.int32, (run, particles), 0)
    one, zero = jnp.ones((), jnp.bfloat16), jnp.zeros((), jnp.bfloat16)

    def steps_from(owner):
        slot_y = lax.rem(row_y - lax.div(owner, side) + side, side)
        slot_x = lax.rem(row_x - lax.rem(owner, side) + side, side)
        return slot_y, slot_x

    def chosen(values, within):
        here = run_id == within
        parts = []
        for f in range(2 * components):
            kept = jnp.where(here, values[f * run : (f + 1) * run], 0.0)
            parts.append(jnp.sum(kept.reshape(run // 8, 8, particles), 0))
        return parts

    def decode(cell):
        line = third(lax.shift_right_logical(cell, 6))
        x = cell - line * x_cells
        source = lax.shift_right_logical(line, 7)
        line = line & (ROWB - 1)
        part = third(lax.shift_right_logical(x, (run // 3).bit_length() - 1))
        within = x - part * run
        return source, part * ROWB + line, within

    @pl.loop(0, blocks)
    def _(b):
        owner = owners[0, row * blocks + b]
        rank = jnp.int32(0)
        for other in range(blocks):
            same = jnp.where(owner_of[other] == owner, 1, 0)
            rank += same * jnp.where(other < b, 1, 0)
        slot_y, slot_x = steps_from(owner)
        source, place, within = decode(cells[slot_y, slot_x])
        weight = weights[slot_x, slot_y]
        offset = offsets[slot_x, slot_y]
        sums = [jnp.zeros((8, particles), jnp.float32) for _ in range(components)]
        for s in range(STEN):
            ones = []
            for start in range(0, XSPLIT * ROWB, depth):
                key = (place[s : s + 1] - start).astype(jnp.bfloat16)
                ones.append(jnp.where(place_id == key, one, zero))
            values = jnp.dot(
                fields[b], jnp.concatenate(ones, 0), preferred_element_type=jnp.float32
            )
            parts = chosen(values, within[s : s + 1])
            for c in range(components):
                sums[c] += weight[s : s + 1] * (parts[c] + offset * parts[components + c])
        mine = source[0:1] == row * CAP + rank
        for c in range(components):
            total = jnp.sum(sums[c], 0, keepdims=True)
            result[b, c : c + 1, :] = jnp.where(mine, total, 0.0)

    for step in [*farthest_first, 0]:
        to = peer(step)
        total = jnp.zeros(result.shape[1:], jnp.float32)
        for b in range(blocks):
            total += result[b] * jnp.where(owner_of[b] == to, 1.0, 0.0)
        back_out[step] = total
    for step in farthest_first:
        give_back(step).start()

    @pl.loop(1, peers)
    def _(step):
        give_back(step).wait()

    total = back_out[0]
    for step in range(1, peers):
        total += back_in[step]
    lane = lax.broadcasted_iota(jnp.int32, (1, PSIZE), 1)
    alive = jnp.concatenate(
        [jnp.where(lane < live[0, k], 1, 0) for k in range(particles // PSIZE)], 1
    )
    old = particle[...]
    total = jnp.where(alive == 1, total, 0.0)
    fluid[...] = total
    updated[...] = jnp.where(alive == 1, old + relax[...] * (total - old), old)
    for way in range(2):
        halo_copy(way).wait_send()
    for entry in shared:
        for k in near_first:
            share(entry, k).wait_send()
            share_line(entry, k).wait_send()


def put_out(grad, fluid, updated, grad_out, fluid_out, updated_out, sems):
    pairs = [(fluid, fluid_out), (updated, updated_out)]
    rows = grad.shape[1] // PIECES
    for c in range(grad.shape[0]):
        for k in range(PIECES):
            piece = (c, pl.ds(k * rows, rows))
            pairs.append((grad.at[piece], grad_out.at[piece]))
    copies = [pltpu.make_async_copy(*pair, sems.at[i]) for i, pair in enumerate(pairs)]
    for copy in copies:
        copy.start()
    for copy in copies:
        copy.wait()


def per_device(
    ring,
    side,
    velocity,
    row_owner,
    cell_list,
    weights,
    offsets,
    relax_rate,
    particle_velocity,
    live_counts,
):
    components, x_cells, lines = velocity.shape
    blocks = lines // ROWB
    particles = weights.shape[1]
    peers = side * side
    run = x_cells // XSPLIT
    far = pl.BlockSpec(memory_space=pltpu.HBM)
    near = pl.BlockSpec(memory_space=pltpu.VMEM)
    dma = pltpu.SemaphoreType.DMA
    results = pl.pallas_call(
        functools.partial(kernel, ring, side),
        out_shape=(
            jax.ShapeDtypeStruct(velocity.shape, jnp.float32),
            jax.ShapeDtypeStruct((components, particles), jnp.float32),
            jax.ShapeDtypeStruct((components, particles), jnp.float32),
        ),
        in_specs=[far] * 10,
        out_specs=(near, near, near),
        scratch_shapes=[
            pltpu.SMEM(row_owner.shape, jnp.int32),
            pltpu.VMEM(velocity.shape, jnp.float32),
            pltpu.VMEM((2, x_cells, x_cells), jnp.bfloat16),
            pltpu.VMEM((x_cells, ROWB), jnp.float32),
            pltpu.VMEM((blocks, 2 * components * run, XSPLIT * ROWB), jnp.bfloat16),
            pltpu.VMEM((2, 8, lines), jnp.float32),
            pltpu.VMEM((2, 8, lines), jnp.float32),
            pltpu.VMEM((side, side, STEN, particles), jnp.int32),
            pltpu.VMEM((side, side, STEN, particles), jnp.float32),
            pltpu.VMEM((side, side, 1, particles), jnp.float32),
            pltpu.VMEM((1, particles), jnp.float32),
            pltpu.VMEM((components, particles), jnp.float32),
            pltpu.SMEM((1, particles // PSIZE), jnp.int32),
            pltpu.VMEM((blocks, components, particles), jnp.float32),
            pltpu.VMEM((peers, components, particles), jnp.float32),
            pltpu.VMEM((peers, components, particles), jnp.float32),
            pltpu.SemaphoreType.REGULAR((2,)),
            dma((12,)),
            dma((2,)),
            dma((2,)),
        ]
        + [dma((2, side))] * 6
        + [dma((peers,))] * 2,
        compiler_params=pltpu.CompilerParams(
            collective_id=0, has_side_effects=True, vmem_limit_bytes=48 * 1024 * 1024
        ),
    )(
        *(
            pltpu.with_memory_space_constraint(array, pltpu.HBM)
            for array in (
                row_owner,
                velocity,
                cell_list,
                weights,
                offsets[None],
                relax_rate[None],
                particle_velocity,
                live_counts[None],
                jnp.asarray(response_matrix(x_cells)),
                jnp.asarray(decay_table(x_cells)),
            )
        ),
    )
    return pl.pallas_call(
        put_out,
        out_shape=tuple(jax.ShapeDtypeStruct(r.shape, r.dtype) for r in results),
        in_specs=[pl.BlockSpec(memory_space=pl.ANY)] * 3,
        out_specs=(far,) * 3,
        scratch_shapes=[dma((2 + components * PIECES,))],
        compiler_params=pltpu.CompilerParams(vmem_limit_bytes=4 * 1024 * 1024),
    )(*results)


def solution(mesh):
    side = math.isqrt(mesh.shape["gy"])
    return jax.shard_map(
        functools.partial(per_device, mesh.shape["gx"], side),
        mesh=mesh,
        in_specs=(
            P(None, "gx", "gy"),
            P("gx", None),
            P(None, ("gx", "gy")),
            P(None, ("gx", "gy")),
            P(("gx", "gy")),
            P(("gx", "gy")),
            P(None, ("gx", "gy")),
            P(("gx", "gy")),
        ),
        out_specs=(P(None, "gx", "gy"), P(None, ("gx", "gy")), P(None, ("gx", "gy"))),
        check_vma=False,
    )
```

```python
import functools
import math

import jax
import jax.numpy as jnp
import numpy as np
from jax import lax
from jax.experimental import pallas as pl
from jax.experimental.pallas import tpu as pltpu
from jax.sharding import PartitionSpec as P

ROWB = 128
PSIZE = 128
CAP = 2
STEN = 4
XSPLIT = 4
PIECES = 1
MESH = pl.DeviceIdType.MESH

DECAY = (3.0 - math.sqrt(5.0)) / 2.0
RATIO = -DECAY
GAIN = 3.0 / math.sqrt(5.0)


def green(distance):
    return GAIN * RATIO ** abs(distance)


def response(d):
    return (7.0 / 9.0) * (green(d + 1) - green(d - 1)) + (1.0 / 36.0) * (green(d + 2) - green(d - 2))


TAIL = response(2) / RATIO**2
NEAR = response(1) - TAIL * RATIO


def response_matrix(x_cells):
    table = np.array([response(d) for d in range(1 - x_cells, x_cells)])
    position = np.arange(x_cells)
    exact = table[position[:, None] - position[None, :] + x_cells - 1]
    high = exact.astype(jnp.bfloat16)
    low = (exact - high.astype(np.float64)).astype(jnp.bfloat16)
    return np.stack([high, low])


def decay_table(x_cells):
    position = np.arange(x_cells)
    powers = RATIO ** np.minimum(position, x_cells - 1 - position).astype(np.float64)
    return np.broadcast_to(powers[:, None], (x_cells, ROWB)).astype(np.float32)


def third(value):
    return lax.shift_right_logical(value * 43691, 17)


def is_equal(value, other):
    return jnp.where(value == other, 1, 0)


def kernel(
    ring,
    side,
    owner_ref,
    vel_ref,
    cells_ref,
    weights_ref,
    offsets_ref,
    relax_ref,
    particle_ref,
    live_ref,
    matrix_ref,
    decay_ref,
    grad,
    fluid,
    updated,
    owners,
    vel,
    matrix,
    decay,
    fields,
    halo_out,
    halo_in,
    cells,
    weights,
    offsets,
    relax,
    particle,
    live,
    result,
    back_out,
    back_in,
    ready,
    load_sem,
    halo_send,
    halo_recv,
    cell_send,
    cell_recv,
    weight_send,
    weight_recv,
    offset_send,
    offset_recv,
    back_send,
    back_recv,
):
    components, x_cells, lines = vel.shape
    blocks = lines // ROWB
    run = x_cells // XSPLIT
    particles = cells.shape[-1]
    peers = side * side
    col = lax.axis_index("gx")
    row = lax.axis_index("gy")
    row_y, row_x = lax.div(row, side), lax.rem(row, side)
    right, left = lax.rem(col + 1, ring), lax.rem(col + ring - 1, ring)

    def peer(step):
        y = lax.rem(row_y + lax.div(step, side), side)
        x = lax.rem(row_x + lax.rem(step, side), side)
        return y * side + x

    near_first = sorted(range(1, side), key=lambda k: -min(k, side - k))

    odd = lax.rem(col, 2)
    first, last, second = is_equal(col, 0), is_equal(col, ring - 1), is_equal(col, 1)
    leads = (
        first + odd * (1 - last) * (1 - first),
        first + odd * (1 - second) * (1 - first),
    )
    beside = (right, left)

    barrier = pltpu.get_barrier_semaphore()

    for k in near_first:
        for step in (k, k * side):
            pl.semaphore_signal(
                barrier, inc=1, device_id=(col, peer(step)), device_id_type=MESH
            )
    for way in range(2):

        @pl.when(leads[way] == 1)
        def _(way=way):
            pl.semaphore_signal(
                barrier, inc=1, device_id=(beside[way], row), device_id_type=MESH
            )

    edge = (slice(0, run), slice(x_cells - run, x_cells))
    inner = slice(run, x_cells - run)
    loads = [
        pltpu.make_async_copy(source, target, load_sem.at[i])
        for i, (source, target) in enumerate(
            (
                (decay_ref, decay),
                (vel_ref.at[:, edge[0]], vel.at[:, edge[0]]),
                (vel_ref.at[:, edge[1]], vel.at[:, edge[1]]),
                (cells_ref, cells.at[0, 0]),
                (weights_ref, weights.at[0, 0]),
                (offsets_ref, offsets.at[0, 0]),
                (vel_ref.at[:, inner], vel.at[:, inner]),
                (matrix_ref, matrix),
                (owner_ref, owners),
                (relax_ref, relax),
                (particle_ref, particle),
                (live_ref, live),
            )
        )
    ]
    for load in loads:
        load.start()

    def halo_copy(way):
        return pltpu.make_async_remote_copy(
            src_ref=halo_out.at[way],
            dst_ref=halo_in.at[way],
            send_sem=halo_send.at[way],
            recv_sem=halo_recv.at[way],
            device_id=(beside[way], row),
            device_id_type=MESH,
        )

    def share(entry, k):
        source, array, first, send_sem, recv_sem = entry
        return pltpu.make_async_remote_copy(
            src_ref=source,
            dst_ref=array.at[0, k],
            send_sem=send_sem.at[0, k],
            recv_sem=recv_sem.at[0, k],
            device_id=(col, peer(k * first)),
            device_id_type=MESH,
        )

    def share_line(entry, k):
        _, array, first, send_sem, recv_sem = entry
        return pltpu.make_async_remote_copy(
            src_ref=array.at[0],
            dst_ref=array.at[k],
            send_sem=send_sem.at[1, k],
            recv_sem=recv_sem.at[1, k],
            device_id=(col, peer(k * side // first)),
            device_id_type=MESH,
        )

    def give_back(step):
        return pltpu.make_async_remote_copy(
            src_ref=back_out.at[step],
            dst_ref=back_in.at[step],
            send_sem=back_send.at[step],
            recv_sem=back_recv.at[step],
            device_id=(col, peer(step)),
            device_id_type=MESH,
        )

    def hops(step):
        return sum(min(k, side - k) for k in divmod(step, side))

    farthest_first = sorted(range(1, peers), key=hops, reverse=True)
    shared = (
        (cells_ref, cells, 1, cell_send, cell_recv),
        (weights_ref, weights, side, weight_send, weight_recv),
        (offsets_ref, offsets, side, offset_send, offset_recv),
    )
    pl.semaphore_wait(barrier, 2 * (side - 1) + 2 - leads[0] - leads[1])
    for entry in shared:
        for k in near_first:
            share(entry, k).start()
    for way in range(2):

        @pl.when(leads[way] == 0)
        def _(way=way):
            pl.semaphore_signal(
                ready.at[1 - way], inc=1, device_id=(beside[way], row), device_id_type=MESH
            )

    for load in loads[:3]:
        load.wait()
    for c in range(components):
        for b in range(blocks):
            lanes = slice(b * ROWB, (b + 1) * ROWB)
            for way in range(2):
                rows = edge[1 - way]
                halo_out[way, c : c + 1, lanes] = jnp.sum(
                    vel[c, rows, lanes] * decay[rows, :], 0, keepdims=True
                )
        halo_out[0, 4 + c : 5 + c, :] = vel[c, x_cells - 1 : x_cells, :]
        halo_out[1, 4 + c : 5 + c, :] = vel[c, 0:1, :]

    for way in range(2):

        @pl.when(leads[way] == 0)
        def _(way=way):
            halo_copy(way).start()

    for load in loads[3:6]:
        load.wait()
    for entry in shared:
        for k in near_first:
            share(entry, k).wait_recv()
        for k in near_first:
            share_line(entry, k).start()

    for load in loads[6:]:
        load.wait()
    for c in range(components):
        value = vel[c]
        high = value.astype(jnp.bfloat16)
        low = (value - high.astype(jnp.float32)).astype(jnp.bfloat16)
        dot = functools.partial(jnp.dot, preferred_element_type=jnp.float32)
        total = dot(matrix[0], high) + (dot(matrix[0], low) + dot(matrix[1], high))
        grad[c] = total
        rounded = total.astype(jnp.bfloat16)
        for b in range(blocks):
            lanes = slice(b * ROWB, (b + 1) * ROWB)
            for part in range(XSPLIT):
                rows = slice(part * run, (part + 1) * run)
                place = slice(part * ROWB, (part + 1) * ROWB)
                fields[b, c * run : (c + 1) * run, place] = high[rows, lanes]
                if 0 < part < XSPLIT - 1:
                    d = components + c
                    fields[b, d * run : (d + 1) * run, place] = rounded[rows, lanes]

    for way in range(2):

        @pl.when(leads[way] == 1)
        def _(way=way):
            pl.semaphore_wait(ready.at[way], 1)
            halo_copy(way).start()

    for way in range(2):
        halo_copy(way).wait_recv()
    for c in range(components):
        for way, end, sign in ((0, 0, 1.0), (1, x_cells - 1, -1.0)):
            grad[c, end : end + 1, :] += (sign * NEAR) * halo_in[way, 4 + c : 5 + c, :]
            for b in range(blocks):
                lanes = slice(b * ROWB, (b + 1) * ROWB)
                far = (sign * TAIL * RATIO) * halo_in[way, c : c + 1, lanes]
                total = grad[c, edge[way], lanes] + decay[edge[way], :] * far
                grad[c, edge[way], lanes] = total
                part = way * (XSPLIT - 1)
                d = components + c
                fields[b, d * run : (d + 1) * run, part * ROWB : (part + 1) * ROWB] = total.astype(
                    jnp.bfloat16
                )

    for entry in shared:
        for k in near_first:
            share_line(entry, k).wait_recv()

    owner_of = [owners[0, row * blocks + b] for b in range(blocks)]
    depth = 2 * ROWB
    place_id = lax.broadcasted_iota(jnp.int32, (depth, particles), 0).astype(jnp.bfloat16)
    run_id = lax.broadcasted_iota(jnp.int32, (run, particles), 0)
    one, zero = jnp.ones((), jnp.bfloat16), jnp.zeros((), jnp.bfloat16)

    def steps_from(owner):
        slot_y = lax.rem(row_y - lax.div(owner, side) + side, side)
        slot_x = lax.rem(row_x - lax.rem(owner, side) + side, side)
        return slot_y, slot_x

    def chosen(values, within):
        here = run_id == within
        parts = []
        for f in range(2 * components):
            kept = jnp.where(here, values[f * run : (f + 1) * run], 0.0)
            parts.append(jnp.sum(kept.reshape(run // 8, 8, particles), 0))
        return parts

    def decode(cell):
        line = third(lax.shift_right_logical(cell, 6))
        x = cell - line * x_cells
        source = lax.shift_right_logical(line, 7)
        line = line & (ROWB - 1)
        part = third(lax.shift_right_logical(x, (run // 3).bit_length() - 1))
        within = x - part * run
        return source, part * ROWB + line, within

    @pl.loop(0, blocks)
    def _(b):
        owner = owners[0, row * blocks + b]
        rank = jnp.int32(0)
        for other in range(blocks):
            same = jnp.where(owner_of[other] == owner, 1, 0)
            rank += same * jnp.where(other < b, 1, 0)
        slot_y, slot_x = steps_from(owner)
        source, place, within = decode(cells[slot_y, slot_x])
        weight = weights[slot_x, slot_y]
        offset = offsets[slot_x, slot_y]
        sums = [jnp.zeros((8, particles), jnp.float32) for _ in range(components)]
        for s in range(STEN):
            ones = []
            for start in range(0, XSPLIT * ROWB, depth):
                key = (place[s : s + 1] - start).astype(jnp.bfloat16)
                ones.append(jnp.where(place_id == key, one, zero))
            values = jnp.dot(
                fields[b], jnp.concatenate(ones, 0), preferred_element_type=jnp.float32
            )
            parts = chosen(values, within[s : s + 1])
            for c in range(components):
                sums[c] += weight[s : s + 1] * (parts[c] + offset * parts[components + c])
        mine = source[0:1] == row * CAP + rank
        for c in range(components):
            total = jnp.sum(sums[c], 0, keepdims=True)
            result[b, c : c + 1, :] = jnp.where(mine, total, 0.0)

    for step in [*farthest_first, 0]:
        to = peer(step)
        total = jnp.zeros(result.shape[1:], jnp.float32)
        for b in range(blocks):
            total += result[b] * jnp.where(owner_of[b] == to, 1.0, 0.0)
        back_out[step] = total
    for step in farthest_first:
        give_back(step).start()

    for way in range(2):
        halo_copy(way).wait_send()
    for entry in shared:
        for k in near_first:
            share(entry, k).wait_send()
            share_line(entry, k).wait_send()
    lane = lax.broadcasted_iota(jnp.int32, (1, PSIZE), 1)
    alive = jnp.concatenate(
        [jnp.where(lane < live[0, k], 1, 0) for k in range(particles // PSIZE)], 1
    )
    old = particle[...]
    rate = relax[...]
    total = back_out[0]
    for step in reversed(farthest_first):
        give_back(step).wait_send()
    for step in reversed(farthest_first):
        give_back(step).wait_recv()
        total += back_in[step]
    total = jnp.where(alive == 1, total, 0.0)
    fluid[...] = total
    updated[...] = jnp.where(alive == 1, old + rate * (total - old), old)


def put_out(grad, fluid, updated, grad_out, fluid_out, updated_out, sems):
    pairs = [(fluid, fluid_out), (updated, updated_out)]
    rows = grad.shape[1] // PIECES
    for c in range(grad.shape[0]):
        for k in range(PIECES):
            piece = (c, pl.ds(k * rows, rows))
            pairs.append((grad.at[piece], grad_out.at[piece]))
    copies = [pltpu.make_async_copy(*pair, sems.at[i]) for i, pair in enumerate(pairs)]
    for copy in copies:
        copy.start()
    for copy in copies:
        copy.wait()


def per_device(
    ring,
    side,
    velocity,
    row_owner,
    cell_list,
    weights,
    offsets,
    relax_rate,
    particle_velocity,
    live_counts,
):
    components, x_cells, lines = velocity.shape
    blocks = lines // ROWB
    particles = weights.shape[1]
    peers = side * side
    run = x_cells // XSPLIT
    far = pl.BlockSpec(memory_space=pltpu.HBM)
    near = pl.BlockSpec(memory_space=pltpu.VMEM)
    dma = pltpu.SemaphoreType.DMA
    results = pl.pallas_call(
        functools.partial(kernel, ring, side),
        out_shape=(
            jax.ShapeDtypeStruct(velocity.shape, jnp.float32),
            jax.ShapeDtypeStruct((components, particles), jnp.float32),
            jax.ShapeDtypeStruct((components, particles), jnp.float32),
        ),
        in_specs=[far] * 10,
        out_specs=(near, near, near),
        scratch_shapes=[
            pltpu.SMEM(row_owner.shape, jnp.int32),
            pltpu.VMEM(velocity.shape, jnp.float32),
            pltpu.VMEM((2, x_cells, x_cells), jnp.bfloat16),
            pltpu.VMEM((x_cells, ROWB), jnp.float32),
            pltpu.VMEM((blocks, 2 * components * run, XSPLIT * ROWB), jnp.bfloat16),
            pltpu.VMEM((2, 8, lines), jnp.float32),
            pltpu.VMEM((2, 8, lines), jnp.float32),
            pltpu.VMEM((side, side, STEN, particles), jnp.int32),
            pltpu.VMEM((side, side, STEN, particles), jnp.float32),
            pltpu.VMEM((side, side, 1, particles), jnp.float32),
            pltpu.VMEM((1, particles), jnp.float32),
            pltpu.VMEM((components, particles), jnp.float32),
            pltpu.SMEM((1, particles // PSIZE), jnp.int32),
            pltpu.VMEM((blocks, components, particles), jnp.float32),
            pltpu.VMEM((peers, components, particles), jnp.float32),
            pltpu.VMEM((peers, components, particles), jnp.float32),
            pltpu.SemaphoreType.REGULAR((2,)),
            dma((12,)),
            dma((2,)),
            dma((2,)),
        ]
        + [dma((2, side))] * 6
        + [dma((peers,))] * 2,
        compiler_params=pltpu.CompilerParams(
            collective_id=0, has_side_effects=True, vmem_limit_bytes=48 * 1024 * 1024
        ),
    )(
        *(
            pltpu.with_memory_space_constraint(array, pltpu.HBM)
            for array in (
                row_owner,
                velocity,
                cell_list,
                weights,
                offsets[None],
                relax_rate[None],
                particle_velocity,
                live_counts[None],
                jnp.asarray(response_matrix(x_cells)),
                jnp.asarray(decay_table(x_cells)),
            )
        ),
    )
    return pl.pallas_call(
        put_out,
        out_shape=tuple(jax.ShapeDtypeStruct(r.shape, r.dtype) for r in results),
        in_specs=[pl.BlockSpec(memory_space=pl.ANY)] * 3,
        out_specs=(far,) * 3,
        scratch_shapes=[dma((2 + components * PIECES,))],
        compiler_params=pltpu.CompilerParams(vmem_limit_bytes=4 * 1024 * 1024),
    )(*results)


def solution(mesh):
    side = math.isqrt(mesh.shape["gy"])
    return jax.shard_map(
        functools.partial(per_device, mesh.shape["gx"], side),
        mesh=mesh,
        in_specs=(
            P(None, "gx", "gy"),
            P("gx", None),
            P(None, ("gx", "gy")),
            P(None, ("gx", "gy")),
            P(("gx", "gy")),
            P(("gx", "gy")),
            P(None, ("gx", "gy")),
            P(("gx", "gy")),
        ),
        out_specs=(P(None, "gx", "gy"), P(None, ("gx", "gy")), P(None, ("gx", "gy"))),
        check_vma=False,
    )
```

```python
import functools
import math

import jax
import jax.numpy as jnp
import numpy as np
from jax import lax
from jax.experimental import pallas as pl
from jax.experimental.pallas import tpu as pltpu
from jax.sharding import PartitionSpec as P

ROWB = 128
PSIZE = 128
CAP = 2
STEN = 4
XSPLIT = 4
PIECES = 1
MESH = pl.DeviceIdType.MESH

DECAY = (3.0 - math.sqrt(5.0)) / 2.0
RATIO = -DECAY
GAIN = 3.0 / math.sqrt(5.0)


def green(distance):
    return GAIN * RATIO ** abs(distance)


def response(d):
    return (7.0 / 9.0) * (green(d + 1) - green(d - 1)) + (1.0 / 36.0) * (green(d + 2) - green(d - 2))


TAIL = response(2) / RATIO**2
NEAR = response(1) - TAIL * RATIO


def response_matrix(x_cells):
    table = np.array([response(d) for d in range(1 - x_cells, x_cells)])
    position = np.arange(x_cells)
    exact = table[position[:, None] - position[None, :] + x_cells - 1]
    high = exact.astype(jnp.bfloat16)
    low = (exact - high.astype(np.float64)).astype(jnp.bfloat16)
    return np.stack([high, low])


def decay_table(x_cells):
    position = np.arange(x_cells)
    powers = RATIO ** np.minimum(position, x_cells - 1 - position).astype(np.float64)
    return np.broadcast_to(powers[:, None], (x_cells, ROWB)).astype(np.float32)


def third(value):
    return lax.shift_right_logical(value * 43691, 17)


def is_equal(value, other):
    return jnp.where(value == other, 1, 0)


def kernel(
    ring,
    side,
    owner_ref,
    vel_ref,
    cells_ref,
    weights_ref,
    offsets_ref,
    relax_ref,
    particle_ref,
    live_ref,
    matrix_ref,
    decay_ref,
    grad,
    fluid,
    updated,
    owners,
    vel,
    matrix,
    decay,
    fields,
    halo_out,
    halo_in,
    cells,
    weights,
    offsets,
    relax,
    particle,
    live,
    result,
    back_out,
    back_in,
    ready,
    load_sem,
    halo_send,
    halo_recv,
    cell_send,
    cell_recv,
    weight_send,
    weight_recv,
    offset_send,
    offset_recv,
    back_send,
    back_recv,
):
    components, x_cells, lines = vel.shape
    blocks = lines // ROWB
    run = x_cells // XSPLIT
    particles = cells.shape[-1]
    peers = side * side
    col = lax.axis_index("gx")
    row = lax.axis_index("gy")
    row_y, row_x = lax.div(row, side), lax.rem(row, side)
    right, left = lax.rem(col + 1, ring), lax.rem(col + ring - 1, ring)

    def peer(step):
        y = lax.rem(row_y + lax.div(step, side), side)
        x = lax.rem(row_x + lax.rem(step, side), side)
        return y * side + x

    near_first = sorted(range(1, side), key=lambda k: -min(k, side - k))

    odd = lax.rem(col, 2)
    first, last, second = is_equal(col, 0), is_equal(col, ring - 1), is_equal(col, 1)
    leads = (
        first + odd * (1 - last) * (1 - first),
        first + odd * (1 - second) * (1 - first),
    )
    beside = (right, left)

    barrier = pltpu.get_barrier_semaphore()

    for k in near_first:
        for step in (k, k * side):
            pl.semaphore_signal(
                barrier, inc=1, device_id=(col, peer(step)), device_id_type=MESH
            )
    for way in range(2):

        @pl.when(leads[way] == 1)
        def _(way=way):
            pl.semaphore_signal(
                barrier, inc=1, device_id=(beside[way], row), device_id_type=MESH
            )

    edge = (slice(0, run), slice(x_cells - run, x_cells))
    inner = slice(run, x_cells - run)
    loads = [
        pltpu.make_async_copy(source, target, load_sem.at[i])
        for i, (source, target) in enumerate(
            (
                (decay_ref, decay),
                (vel_ref.at[:, edge[0]], vel.at[:, edge[0]]),
                (vel_ref.at[:, edge[1]], vel.at[:, edge[1]]),
                (cells_ref, cells.at[0, 0]),
                (weights_ref, weights.at[0, 0]),
                (offsets_ref, offsets.at[0, 0]),
                (vel_ref.at[:, inner], vel.at[:, inner]),
                (matrix_ref, matrix),
                (owner_ref, owners),
                (relax_ref, relax),
                (particle_ref, particle),
                (live_ref, live),
            )
        )
    ]
    for load in loads:
        load.start()

    def halo_copy(way):
        return pltpu.make_async_remote_copy(
            src_ref=halo_out.at[way],
            dst_ref=halo_in.at[way],
            send_sem=halo_send.at[way],
            recv_sem=halo_recv.at[way],
            device_id=(beside[way], row),
            device_id_type=MESH,
        )

    def share(entry, k):
        source, array, first, send_sem, recv_sem = entry
        return pltpu.make_async_remote_copy(
            src_ref=source,
            dst_ref=array.at[0, k],
            send_sem=send_sem.at[0, k],
            recv_sem=recv_sem.at[0, k],
            device_id=(col, peer(k * first)),
            device_id_type=MESH,
        )

    def share_line(entry, k):
        _, array, first, send_sem, recv_sem = entry
        return pltpu.make_async_remote_copy(
            src_ref=array.at[0],
            dst_ref=array.at[k],
            send_sem=send_sem.at[1, k],
            recv_sem=recv_sem.at[1, k],
            device_id=(col, peer(k * side // first)),
            device_id_type=MESH,
        )

    def give_back(step):
        return pltpu.make_async_remote_copy(
            src_ref=back_out.at[step],
            dst_ref=back_in.at[step],
            send_sem=back_send.at[step],
            recv_sem=back_recv.at[step],
            device_id=(col, peer(step)),
            device_id_type=MESH,
        )

    def hops(step):
        return sum(min(k, side - k) for k in divmod(step, side))

    farthest_first = sorted(range(1, peers), key=hops, reverse=True)
    shared = (
        (cells_ref, cells, 1, cell_send, cell_recv),
        (weights_ref, weights, side, weight_send, weight_recv),
        (offsets_ref, offsets, side, offset_send, offset_recv),
    )
    pl.semaphore_wait(barrier, 2 * (side - 1) + 2 - leads[0] - leads[1])
    for entry in shared:
        for k in near_first:
            share(entry, k).start()
    for way in range(2):

        @pl.when(leads[way] == 0)
        def _(way=way):
            pl.semaphore_signal(
                ready.at[1 - way], inc=1, device_id=(beside[way], row), device_id_type=MESH
            )

    for load in loads[:3]:
        load.wait()
    for c in range(components):
        for b in range(blocks):
            lanes = slice(b * ROWB, (b + 1) * ROWB)
            for way in range(2):
                rows = edge[1 - way]
                halo_out[way, c : c + 1, lanes] = jnp.sum(
                    vel[c, rows, lanes] * decay[rows, :], 0, keepdims=True
                )
        halo_out[0, 4 + c : 5 + c, :] = vel[c, x_cells - 1 : x_cells, :]
        halo_out[1, 4 + c : 5 + c, :] = vel[c, 0:1, :]

    for way in range(2):

        @pl.when(leads[way] == 0)
        def _(way=way):
            halo_copy(way).start()

    for load in loads[3:6]:
        load.wait()
    for entry in shared:
        for k in near_first:
            share(entry, k).wait_recv()
        for k in near_first:
            share_line(entry, k).start()

    for load in loads[6:]:
        load.wait()
    for c in range(components):
        value = vel[c]
        high = value.astype(jnp.bfloat16)
        low = (value - high.astype(jnp.float32)).astype(jnp.bfloat16)
        dot = functools.partial(jnp.dot, preferred_element_type=jnp.float32)
        total = dot(matrix[0], high) + (dot(matrix[0], low) + dot(matrix[1], high))
        grad[c] = total
        rounded = total.astype(jnp.bfloat16)
        for b in range(blocks):
            lanes = slice(b * ROWB, (b + 1) * ROWB)
            for part in range(XSPLIT):
                rows = slice(part * run, (part + 1) * run)
                place = slice(part * ROWB, (part + 1) * ROWB)
                fields[b, c * run : (c + 1) * run, place] = high[rows, lanes]
                if 0 < part < XSPLIT - 1:
                    d = components + c
                    fields[b, d * run : (d + 1) * run, place] = rounded[rows, lanes]

    for way in range(2):

        @pl.when(leads[way] == 1)
        def _(way=way):
            pl.semaphore_wait(ready.at[way], 1)
            halo_copy(way).start()

    for way in range(2):
        halo_copy(way).wait_recv()
    for c in range(components):
        for way, end, sign in ((0, 0, 1.0), (1, x_cells - 1, -1.0)):
            grad[c, end : end + 1, :] += (sign * NEAR) * halo_in[way, 4 + c : 5 + c, :]
            for b in range(blocks):
                lanes = slice(b * ROWB, (b + 1) * ROWB)
                far = (sign * TAIL * RATIO) * halo_in[way, c : c + 1, lanes]
                total = grad[c, edge[way], lanes] + decay[edge[way], :] * far
                grad[c, edge[way], lanes] = total
                part = way * (XSPLIT - 1)
                d = components + c
                fields[b, d * run : (d + 1) * run, part * ROWB : (part + 1) * ROWB] = total.astype(
                    jnp.bfloat16
                )

    for entry in shared:
        for k in near_first:
            share_line(entry, k).wait_recv()

    owner_of = [owners[0, row * blocks + b] for b in range(blocks)]
    depth = 2 * ROWB
    place_id = lax.broadcasted_iota(jnp.int32, (depth, particles), 0).astype(jnp.bfloat16)
    run_id = lax.broadcasted_iota(jnp.int32, (run, particles), 0)
    one, zero = jnp.ones((), jnp.bfloat16), jnp.zeros((), jnp.bfloat16)

    def steps_from(owner):
        slot_y = lax.rem(row_y - lax.div(owner, side) + side, side)
        slot_x = lax.rem(row_x - lax.rem(owner, side) + side, side)
        return slot_y, slot_x

    def chosen(values, within):
        here = run_id == within
        parts = []
        for f in range(2 * components):
            kept = jnp.where(here, values[f * run : (f + 1) * run], 0.0)
            parts.append(jnp.sum(kept.reshape(run // 8, 8, particles), 0))
        return parts

    def decode(cell):
        line = third(lax.shift_right_logical(cell, 6))
        x = cell - line * x_cells
        source = lax.shift_right_logical(line, 7)
        line = line & (ROWB - 1)
        part = third(lax.shift_right_logical(x, (run // 3).bit_length() - 1))
        within = x - part * run
        return source, part * ROWB + line, within

    @pl.loop(0, blocks)
    def _(b):
        owner = owners[0, row * blocks + b]
        rank = jnp.int32(0)
        for other in range(blocks):
            same = jnp.where(owner_of[other] == owner, 1, 0)
            rank += same * jnp.where(other < b, 1, 0)
        slot_y, slot_x = steps_from(owner)
        source, place, within = decode(cells[slot_y, slot_x])
        weight = weights[slot_x, slot_y]
        offset = offsets[slot_x, slot_y]
        sums = [jnp.zeros((8, particles), jnp.float32) for _ in range(components)]
        for s in range(STEN):
            ones = []
            for start in range(0, XSPLIT * ROWB, depth):
                key = (place[s : s + 1] - start).astype(jnp.bfloat16)
                ones.append(jnp.where(place_id == key, one, zero))
            values = jnp.dot(
                fields[b], jnp.concatenate(ones, 0), preferred_element_type=jnp.float32
            )
            parts = chosen(values, within[s : s + 1])
            for c in range(components):
                sums[c] += weight[s : s + 1] * (parts[c] + offset * parts[components + c])
        mine = source[0:1] == row * CAP + rank
        for c in range(components):
            total = jnp.sum(sums[c], 0, keepdims=True)
            result[b, c : c + 1, :] = jnp.where(mine, total, 0.0)

    lag = 6
    for i, step in enumerate([*farthest_first, 0]):
        to = peer(step)
        total = jnp.zeros(result.shape[1:], jnp.float32)
        for b in range(blocks):
            total += result[b] * jnp.where(owner_of[b] == to, 1.0, 0.0)
        back_out[step] = total
        if i >= lag:
            give_back(farthest_first[i - lag]).start()
    for step in farthest_first[max(peers - lag, 0) :]:
        give_back(step).start()

    for way in range(2):
        halo_copy(way).wait_send()
    for entry in shared:
        for k in near_first:
            share(entry, k).wait_send()
            share_line(entry, k).wait_send()
    lane = lax.broadcasted_iota(jnp.int32, (1, PSIZE), 1)
    alive = jnp.concatenate(
        [jnp.where(lane < live[0, k], 1, 0) for k in range(particles // PSIZE)], 1
    )
    old = particle[...]
    rate = relax[...]
    total = back_out[0]
    for step in reversed(farthest_first):
        give_back(step).wait_send()
    for step in reversed(farthest_first):
        give_back(step).wait_recv()
        total += back_in[step]
    total = jnp.where(alive == 1, total, 0.0)
    fluid[...] = total
    updated[...] = jnp.where(alive == 1, old + rate * (total - old), old)


def put_out(grad, fluid, updated, grad_out, fluid_out, updated_out, sems):
    pairs = [(fluid, fluid_out), (updated, updated_out)]
    rows = grad.shape[1] // PIECES
    for c in range(grad.shape[0]):
        for k in range(PIECES):
            piece = (c, pl.ds(k * rows, rows))
            pairs.append((grad.at[piece], grad_out.at[piece]))
    copies = [pltpu.make_async_copy(*pair, sems.at[i]) for i, pair in enumerate(pairs)]
    for copy in copies:
        copy.start()
    for copy in copies:
        copy.wait()


def per_device(
    ring,
    side,
    velocity,
    row_owner,
    cell_list,
    weights,
    offsets,
    relax_rate,
    particle_velocity,
    live_counts,
):
    components, x_cells, lines = velocity.shape
    blocks = lines // ROWB
    particles = weights.shape[1]
    peers = side * side
    run = x_cells // XSPLIT
    far = pl.BlockSpec(memory_space=pltpu.HBM)
    near = pl.BlockSpec(memory_space=pltpu.VMEM)
    dma = pltpu.SemaphoreType.DMA
    results = pl.pallas_call(
        functools.partial(kernel, ring, side),
        out_shape=(
            jax.ShapeDtypeStruct(velocity.shape, jnp.float32),
            jax.ShapeDtypeStruct((components, particles), jnp.float32),
            jax.ShapeDtypeStruct((components, particles), jnp.float32),
        ),
        in_specs=[far] * 10,
        out_specs=(near, near, near),
        scratch_shapes=[
            pltpu.SMEM(row_owner.shape, jnp.int32),
            pltpu.VMEM(velocity.shape, jnp.float32),
            pltpu.VMEM((2, x_cells, x_cells), jnp.bfloat16),
            pltpu.VMEM((x_cells, ROWB), jnp.float32),
            pltpu.VMEM((blocks, 2 * components * run, XSPLIT * ROWB), jnp.bfloat16),
            pltpu.VMEM((2, 8, lines), jnp.float32),
            pltpu.VMEM((2, 8, lines), jnp.float32),
            pltpu.VMEM((side, side, STEN, particles), jnp.int32),
            pltpu.VMEM((side, side, STEN, particles), jnp.float32),
            pltpu.VMEM((side, side, 1, particles), jnp.float32),
            pltpu.VMEM((1, particles), jnp.float32),
            pltpu.VMEM((components, particles), jnp.float32),
            pltpu.SMEM((1, particles // PSIZE), jnp.int32),
            pltpu.VMEM((blocks, components, particles), jnp.float32),
            pltpu.VMEM((peers, components, particles), jnp.float32),
            pltpu.VMEM((peers, components, particles), jnp.float32),
            pltpu.SemaphoreType.REGULAR((2,)),
            dma((12,)),
            dma((2,)),
            dma((2,)),
        ]
        + [dma((2, side))] * 6
        + [dma((peers,))] * 2,
        compiler_params=pltpu.CompilerParams(
            collective_id=0, has_side_effects=True, vmem_limit_bytes=48 * 1024 * 1024
        ),
    )(
        *(
            pltpu.with_memory_space_constraint(array, pltpu.HBM)
            for array in (
                row_owner,
                velocity,
                cell_list,
                weights,
                offsets[None],
                relax_rate[None],
                particle_velocity,
                live_counts[None],
                jnp.asarray(response_matrix(x_cells)),
                jnp.asarray(decay_table(x_cells)),
            )
        ),
    )
    return pl.pallas_call(
        put_out,
        out_shape=tuple(jax.ShapeDtypeStruct(r.shape, r.dtype) for r in results),
        in_specs=[pl.BlockSpec(memory_space=pl.ANY)] * 3,
        out_specs=(far,) * 3,
        scratch_shapes=[dma((2 + components * PIECES,))],
        compiler_params=pltpu.CompilerParams(vmem_limit_bytes=4 * 1024 * 1024),
    )(*results)


def solution(mesh):
    side = math.isqrt(mesh.shape["gy"])
    return jax.shard_map(
        functools.partial(per_device, mesh.shape["gx"], side),
        mesh=mesh,
        in_specs=(
            P(None, "gx", "gy"),
            P("gx", None),
            P(None, ("gx", "gy")),
            P(None, ("gx", "gy")),
            P(("gx", "gy")),
            P(("gx", "gy")),
            P(None, ("gx", "gy")),
            P(("gx", "gy")),
        ),
        out_specs=(P(None, "gx", "gy"), P(None, ("gx", "gy")), P(None, ("gx", "gy"))),
        check_vma=False,
    )
```
